32 devices in a mesh: fsdp: 4 (over y, core), ctx: 8 (over z, x).
Axes of the slice: x: 2, y: 2, z: 4, core: 2. Of those that a mesh axis runs over, the one named last changes fastest.
Arguments:
- query_proj: bfloat16 [4, 1024, 4096], P('fsdp', 'ctx'), may hold values from -10 to 10
- key_proj: bfloat16 [4, 1024, 4096], P('fsdp', 'ctx'), may hold values from -10 to 10
- value_proj: bfloat16 [4, 1024, 4096], P('fsdp', 'ctx'), may hold values from -12 to 12
- modality: int32 [4, 1024], P('fsdp', 'ctx'), may hold values from 0 to 1, as said below
- out_weight: bfloat16 [2, 4096, 2048], P(None, ('fsdp', 'ctx')), may hold values from -0.09375 to 0.09375
- grad_projected: bfloat16 [4, 1024, 2048], P('fsdp', 'ctx'), may hold values from -6 to 6
Outputs:
- projected: bfloat16 [4, 1024, 2048], P('fsdp', 'ctx')
- grad_query: bfloat16 [4, 1024, 4096], P('fsdp', 'ctx')
- grad_key: bfloat16 [4, 1024, 4096], P('fsdp', 'ctx')
- grad_value: bfloat16 [4, 1024, 4096], P('fsdp', 'ctx')
The draws below stay inside these ranges and needn't reach their ends.
Inputs may be any that keep to these rules, and one draw needn't show every extreme that they name: `modality`: each sequence holds exactly two image spans of 256 positions each, one starting within the first half and lying in the first half, the other lying in the second half; all other positions are text, so exactly half of each sequence's positions are image.
All inputs are finite; a program needn't handle non-finite values.
Results may differ from the reference program's by a relative error of at most 0.012.
The reference program's roundings to bfloat16 on the way count: a program that leaves them out, or rounds other values in their place, can miss the bound.
Values may be sent and summed in bfloat16 or wider, within the bound.
A program may use at most 320 MiB of HBM per device.

```python
import jax
import jax.numpy as jnp
from jax import lax

HEAD_COUNT = 32
HEAD_SIZE = 128
OUT_WIDTH = 2048
LENGTH = 1024
IMAGE_SPAN = 256
SEQUENCES = 4


def base_draw(key, offset_tag):
    folded = jax.random.fold_in(key, offset_tag)
    extent = (SEQUENCES, LENGTH, HEAD_COUNT * HEAD_SIZE)
    return jnp.clip(1.3 * jax.random.normal(folded, extent, jnp.float32), -6.0, 6.0)


def draw_query_proj(key, part):
    values = base_draw(key, 11)
    return values.astype(jnp.bfloat16)


def draw_key_proj(key, part):
    values = base_draw(key, 23)
    return values.astype(jnp.bfloat16)


def draw_modality(key, part):
    folded = jax.random.fold_in(key, 5)
    first_key, second_key = jax.random.split(folded, 2)
    first_start = jax.random.randint(first_key, (SEQUENCES,), 0, LENGTH // 2 - IMAGE_SPAN + 1)
    second_start = jax.random.randint(second_key, (SEQUENCES,), LENGTH // 2, LENGTH - IMAGE_SPAN + 1)
    places = jnp.arange(LENGTH)[None, :]
    inside_first = (places >= first_start[:, None]) & (places < first_start[:, None] + IMAGE_SPAN)
    inside_second = (places >= second_start[:, None]) & (places < second_start[:, None] + IMAGE_SPAN)
    return (inside_first | inside_second).astype(jnp.int32)


def block_scale(stream_key, shape, cuts, smallest, top_value):
    gain = 1.0
    for position, blocks in cuts:
        heights = jax.random.uniform(jax.random.fold_in(jax.random.fold_in(stream_key, 6), position), (blocks,), jnp.float32, smallest / len(cuts), top_value / len(cuts))
        gain = gain * jnp.repeat(jnp.exp(heights), shape[position] // blocks).reshape((-1,) + (1,) * (len(shape) - 1 - position))
    return gain


def centred(key, dims, width, reach, cuts=(), kind=jnp.bfloat16):
    values = width * jax.random.normal(key, dims, jnp.float32)
    if cuts:
        values = values * block_scale(key, dims, cuts, -0.22, 0.18)
    return jnp.clip(values, -reach, reach).astype(kind)


def setup_inputs(seed: int = 0) -> dict:
    key_of = jax.random.split(jax.random.key(seed), 7)
    return {
        "query_proj": draw_query_proj(jax.random.fold_in(key_of[6], 71), 0),
        "key_proj": draw_key_proj(jax.random.fold_in(key_of[6], 71), 0),
        "value_proj": centred(key_of[2], (SEQUENCES, LENGTH, HEAD_COUNT * HEAD_SIZE), 2.0, 12.0, ((0, 4), (1, 8))),
        "modality": draw_modality(jax.random.fold_in(key_of[6], 71), 0),
        "out_weight": centred(key_of[4], (2, HEAD_COUNT * HEAD_SIZE, OUT_WIDTH), (HEAD_COUNT * HEAD_SIZE) ** -0.5, 0.09375, ((1, 32),)),
        "grad_projected": centred(key_of[5], (SEQUENCES, LENGTH, OUT_WIDTH), 1.0, 6.0, ((0, 4), (1, 8))),
    }


def block_count(length):
    return max(1, min(8, length // 512))


def rounded(matrix):
    return lax.optimization_barrier(matrix.astype(jnp.bfloat16)).astype(jnp.float32)


def probabilities(query_block, key_prefix, offset):
    scaling = query_block.shape[-1] ** -0.5
    scores = jnp.einsum("qhd,khd->hqk", query_block.astype(jnp.float32), key_prefix.astype(jnp.float32)) * scaling
    query_places = offset + jnp.arange(query_block.shape[0])
    key_places = jnp.arange(key_prefix.shape[0])
    scores = jnp.where(key_places[None, None, :] <= query_places[None, :, None], scores, -jnp.inf)
    highest = jnp.max(scores, axis=-1, keepdims=True)
    raised = jnp.exp(scores - highest)
    return raised / jnp.sum(raised, axis=-1, keepdims=True)


def attend_forward(queries, keys_all, values_all):
    length = queries.shape[0]
    block_rows = length // block_count(length)
    pieces = []
    for block_index in range(length // block_rows):
        offset = block_index * block_rows
        finish = offset + block_rows
        weights = probabilities(queries[offset:finish], keys_all[:finish], offset)
        output = jnp.einsum("hqk,khd->qhd", rounded(weights), values_all[:finish].astype(jnp.float32))
        pieces.append(output.astype(jnp.bfloat16))
    return jnp.concatenate(pieces, axis=0)


def attend_backward(queries, keys_all, values_all, attention, grad_attention):
    length = queries.shape[0]
    block_rows = length // block_count(length)
    scaling = queries.shape[-1] ** -0.5
    grad_keys = jnp.zeros(queries.shape, jnp.float32)
    grad_values = jnp.zeros(queries.shape, jnp.float32)
    query_pieces = []
    for block_index in range(length // block_rows):
        offset = block_index * block_rows
        finish = offset + block_rows
        query_block = queries[offset:finish]
        weights = probabilities(query_block, keys_all[:finish], offset)
        grad_block = grad_attention[offset:finish].astype(jnp.float32)
        attn_block = attention[offset:finish].astype(jnp.float32)
        grad_values = grad_values.at[:finish].add(jnp.einsum("hqk,qhd->khd", rounded(weights), grad_block))
        grad_weights = jnp.einsum("qhd,khd->hqk", grad_block, values_all[:finish].astype(jnp.float32))
        row_delta = jnp.sum(grad_block * attn_block, axis=-1).T[:, :, None]
        grad_scores = rounded(weights * (grad_weights - row_delta) * scaling)
        query_pieces.append(jnp.einsum("hqk,khd->qhd", grad_scores, keys_all[:finish].astype(jnp.float32)).astype(jnp.bfloat16))
        grad_keys = grad_keys.at[:finish].add(jnp.einsum("hqk,qhd->khd", grad_scores, query_block.astype(jnp.float32)))
    return jnp.concatenate(query_pieces, axis=0), grad_keys.astype(jnp.bfloat16), grad_values.astype(jnp.bfloat16)


def reference(query_proj, key_proj, value_proj, modality, out_weight, grad_projected):
    def per_sequence(inputs):
        queries, keys_all, values_all, modal_ids, upstream = inputs
        shaped = (LENGTH, HEAD_COUNT, HEAD_SIZE)
        inner_width = HEAD_COUNT * HEAD_SIZE
        queries = queries.reshape(shaped)
        keys_all = keys_all.reshape(shaped)
        values_all = values_all.reshape(shaped)
        attention = attend_forward(queries, keys_all, values_all)
        flat = attention.reshape(LENGTH, inner_width)
        is_image = (modal_ids == 1)[:, None]
        text_out = jnp.dot(flat, out_weight[0], preferred_element_type=jnp.float32)
        image_out = jnp.dot(flat, out_weight[1], preferred_element_type=jnp.float32)
        result = jnp.where(is_image, image_out, text_out).astype(jnp.bfloat16)
        text_back = jnp.dot(upstream, out_weight[0].T, preferred_element_type=jnp.float32)
        image_back = jnp.dot(upstream, out_weight[1].T, preferred_element_type=jnp.float32)
        grad_attention = jnp.where(is_image, image_back, text_back).astype(jnp.bfloat16).reshape(shaped)
        grad_q, grad_k, grad_v = attend_backward(queries, keys_all, values_all, attention, grad_attention)
        return result, grad_q.reshape(LENGTH, inner_width), grad_k.reshape(LENGTH, inner_width), grad_v.reshape(LENGTH, inner_width)

    projected, grad_query, grad_key, grad_value = lax.map(per_sequence, (query_proj, key_proj, value_proj, modality, grad_projected))
    return (projected, grad_query, grad_key, grad_value)
```

```python
import jax
import jax.numpy as jnp
from jax import lax
from jax.experimental import pallas as pl
from jax.experimental.pallas import tpu as pltpu
from jax.sharding import PartitionSpec as P

HEAD_SIZE = 128


def block_count(length):
    return max(1, min(8, length // 512))


def probabilities(query_block, key_prefix, offset):
    scaling = query_block.shape[-1] ** (-0.5)
    scores = (
        jnp.einsum("hqd,hkd->hqk", query_block, key_prefix, preferred_element_type=jnp.float32)
        * scaling
    )
    query_places = offset + jnp.arange(query_block.shape[1])
    key_places = jnp.arange(key_prefix.shape[1])
    scores = jnp.where(key_places[None, None, :] <= query_places[None, :, None], scores, -jnp.inf)
    highest = jnp.max(scores, axis=-1, keepdims=True)
    raised = jnp.exp(scores - highest)
    return raised / jnp.sum(raised, axis=-1, keepdims=True)


def attend_forward(queries, keys_all, values_all):
    length = queries.shape[1]
    block_rows = length // block_count(length)
    pieces = []
    for block_index in range(length // block_rows):
        offset = block_index * block_rows
        finish = offset + block_rows
        weights = probabilities(queries[:, offset:finish], keys_all[:, :finish], offset).astype(
            jnp.bfloat16
        )
        output = jnp.einsum(
            "hqk,hkd->hqd", weights, values_all[:, :finish], preferred_element_type=jnp.float32
        )
        pieces.append(output.astype(jnp.bfloat16))
    return jnp.concatenate(pieces, axis=1)


def attend_backward(queries, keys_all, values_all, attention, grad_attention):
    length = queries.shape[1]
    block_rows = length // block_count(length)
    scaling = queries.shape[-1] ** (-0.5)
    grad_keys = jnp.zeros(queries.shape, jnp.float32)
    grad_values = jnp.zeros(queries.shape, jnp.float32)
    query_pieces = []
    for block_index in range(length // block_rows):
        offset = block_index * block_rows
        finish = offset + block_rows
        query_block = queries[:, offset:finish]
        weights = probabilities(query_block, keys_all[:, :finish], offset)
        grad_block = grad_attention[:, offset:finish]
        attn_block = attention[:, offset:finish]
        grad_values = grad_values.at[:, :finish].add(
            jnp.einsum(
                "hqk,hqd->hkd",
                weights.astype(jnp.bfloat16),
                grad_block,
                preferred_element_type=jnp.float32,
            )
        )
        grad_weights = jnp.einsum(
            "hqd,hkd->hqk", grad_block, values_all[:, :finish], preferred_element_type=jnp.float32
        )
        row_delta = jnp.sum(
            grad_block.astype(jnp.float32) * attn_block.astype(jnp.float32), axis=-1, keepdims=True
        )
        grad_scores = (weights * (grad_weights - row_delta) * scaling).astype(jnp.bfloat16)
        query_pieces.append(
            jnp.einsum(
                "hqk,hkd->hqd",
                grad_scores,
                keys_all[:, :finish],
                preferred_element_type=jnp.float32,
            ).astype(jnp.bfloat16)
        )
        grad_keys = grad_keys.at[:, :finish].add(
            jnp.einsum("hqk,hqd->hkd", grad_scores, query_block, preferred_element_type=jnp.float32)
        )
    return (
        jnp.concatenate(query_pieces, axis=1),
        grad_keys.astype(jnp.bfloat16),
        grad_values.astype(jnp.bfloat16),
    )


def transposed_product(left, right):
    return lax.dot_general(
        left, right, (((1,), (1,)), ((), ())), preferred_element_type=jnp.float32
    )


def heads_first(flat, length, local_heads):
    return flat.reshape(length, local_heads, HEAD_SIZE).transpose(1, 0, 2)


def heads_last(stacked, length, local_width):
    return stacked.transpose(1, 0, 2).reshape(1, length, local_width)


def per_device_gathered(query_proj, key_proj, value_proj, modality, out_weight, grad_projected):
    context_size = lax.axis_size("ctx")
    row_count = query_proj.shape[1]
    inner_width = query_proj.shape[2]
    length = row_count * context_size
    local_width = inner_width // context_size
    local_heads = local_width // HEAD_SIZE
    head_query, head_key, head_value = (
        lax.all_to_all(query_proj, "ctx", split_axis=2, concat_axis=1, tiled=True),
        lax.all_to_all(key_proj, "ctx", split_axis=2, concat_axis=1, tiled=True),
        lax.all_to_all(value_proj, "ctx", split_axis=2, concat_axis=1, tiled=True),
    )
    head_query = heads_first(head_query, length, local_heads)
    head_key = heads_first(head_key, length, local_heads)
    head_value = heads_first(head_value, length, local_heads)
    attention = attend_forward(head_query, head_key, head_value)
    sending = heads_last(attention, length, local_width)
    attn_rows = lax.all_to_all(sending, "ctx", split_axis=1, concat_axis=2, tiled=True)[0]
    upstream = grad_projected[0]
    weight_piece = lax.all_gather(out_weight, ("fsdp", "ctx"), axis=1, tiled=True)
    text_out = jnp.dot(attn_rows, weight_piece[0], preferred_element_type=jnp.float32)
    image_out = jnp.dot(attn_rows, weight_piece[1], preferred_element_type=jnp.float32)
    text_grad = transposed_product(upstream, weight_piece[0])
    image_grad = transposed_product(upstream, weight_piece[1])
    text_out, image_out, text_grad, image_grad = (text_out, image_out, text_grad, image_grad)
    image_rows = (modality[0] == 1)[:, None]
    projected = jnp.where(image_rows, image_out, text_out).astype(jnp.bfloat16)[None]
    grad_rows = jnp.where(image_rows, image_grad, text_grad).astype(jnp.bfloat16)
    grad_heads = lax.all_to_all(grad_rows[None], "ctx", split_axis=2, concat_axis=1, tiled=True)
    grad_heads = heads_first(grad_heads, length, local_heads)
    grad_q, grad_k, grad_v = attend_backward(
        head_query, head_key, head_value, attention, grad_heads
    )
    grad_query, grad_key, grad_value = (
        lax.all_to_all(
            heads_last(grad_q, length, local_width), "ctx", split_axis=1, concat_axis=2, tiled=True
        ),
        lax.all_to_all(
            heads_last(grad_k, length, local_width), "ctx", split_axis=1, concat_axis=2, tiled=True
        ),
        lax.all_to_all(
            heads_last(grad_v, length, local_width), "ctx", split_axis=1, concat_axis=2, tiled=True
        ),
    )
    return (projected, grad_query, grad_key, grad_value)


def fused_attention_kernel(
    q_ref, k_ref, v_ref, g_ref, a_ref, dq_ref, dk_ref, dv_ref, dk_sum, dv_sum
):
    length = q_ref.shape[0]
    rows = min(256, length)
    scaling = HEAD_SIZE ** (-0.5)
    nt = (((1,), (1,)), ((), ()))
    tn = (((0,), (0,)), ((), ()))
    for block in reversed(range(length // rows)):
        offset = block * rows
        finish = offset + rows
        q = q_ref[offset:finish, :]
        g = g_ref[offset:finish, :]
        k = k_ref[:finish, :]
        v = v_ref[:finish, :]
        scores = lax.dot_general(q, k, nt, preferred_element_type=jnp.float32) * scaling
        places = lax.broadcasted_iota(jnp.int32, scores.shape, 0) + offset
        scores = jnp.where(
            lax.broadcasted_iota(jnp.int32, scores.shape, 1) <= places, scores, -jnp.inf
        )
        raised = jnp.exp(scores - jnp.max(scores, axis=-1, keepdims=True))
        weights = raised * (1.0 / jnp.sum(raised, axis=-1, keepdims=True))
        weights_bf = weights.astype(jnp.bfloat16)
        attention = jnp.dot(weights_bf, v, preferred_element_type=jnp.float32).astype(jnp.bfloat16)
        a_ref[offset:finish, :] = attention
        delta = jnp.sum(
            g.astype(jnp.float32) * attention.astype(jnp.float32), axis=-1, keepdims=True
        )
        grad_weights = lax.dot_general(g, v, nt, preferred_element_type=jnp.float32)
        grad_scores = (weights * (grad_weights - delta) * scaling).astype(jnp.bfloat16)
        dq_ref[offset:finish, :] = jnp.dot(
            grad_scores, k, preferred_element_type=jnp.float32
        ).astype(jnp.bfloat16)
        dk = lax.dot_general(grad_scores, q, tn, preferred_element_type=jnp.float32)
        dv = lax.dot_general(weights_bf, g, tn, preferred_element_type=jnp.float32)
        if finish == length:
            dk_sum[...] = dk
            dv_sum[...] = dv
        else:
            dk_sum[:finish, :] += dk
            dv_sum[:finish, :] += dv
    dk_ref[...] = dk_sum[...].astype(jnp.bfloat16)
    dv_ref[...] = dv_sum[...].astype(jnp.bfloat16)


def fused_attention(q, k, v, g):
    length, width = q.shape
    spec = pl.BlockSpec((length, HEAD_SIZE), lambda h: (0, h))
    return pl.pallas_call(
        fused_attention_kernel,
        grid=(width // HEAD_SIZE,),
        in_specs=[spec] * 4,
        out_specs=[spec] * 4,
        out_shape=[jax.ShapeDtypeStruct(q.shape, jnp.bfloat16)] * 4,
        scratch_shapes=[pltpu.VMEM((length, HEAD_SIZE), jnp.float32)] * 2,
        compiler_params=pltpu.CompilerParams(vmem_limit_bytes=48 * 2**20),
        cost_estimate=pl.CostEstimate(
            flops=9 * length * length * width, bytes_accessed=16 * length * width, transcendentals=0
        ),
    )(q, k, v, g)


def per_device(query_proj, key_proj, value_proj, modality, out_weight, grad_projected):
    context_size = lax.axis_size("ctx")
    groups = lax.axis_size("fsdp")
    row_count = query_proj.shape[1]
    piece = out_weight.shape[1]
    length = row_count * context_size
    width = groups * piece

    def to_heads(flat):
        split = flat[0].reshape(row_count, groups, context_size, piece).transpose(2, 0, 1, 3)
        return lax.all_to_all(split, "ctx", 0, 0).reshape(length, width)

    def to_rows(flat):
        split = lax.all_to_all(
            flat.reshape(context_size, row_count, groups, piece), "ctx", 0, 0
        )
        return split.transpose(1, 2, 0, 3).reshape(1, row_count, width * context_size)

    weight = lax.all_gather(out_weight, "fsdp", axis=1, tiled=True).reshape(2 * width, -1)
    upstream = lax.all_gather(grad_projected[0], "ctx", axis=0, tiled=True)
    image = (lax.all_gather(modality[0], "ctx", axis=0, tiled=True) == 1)[:, None]
    both = transposed_product(upstream, weight)
    grad_attention = jnp.where(image, both[:, width:], both[:, :width]).astype(jnp.bfloat16)
    attention, grad_q, grad_k, grad_v = fused_attention(
        to_heads(query_proj), to_heads(key_proj), to_heads(value_proj), grad_attention
    )
    zero = jnp.zeros_like(attention)
    spread = jnp.concatenate(
        [jnp.where(image, zero, attention), jnp.where(image, attention, zero)], axis=1
    )
    partial = jnp.dot(spread, weight, preferred_element_type=jnp.float32).astype(jnp.bfloat16)
    partial = lax.all_to_all(partial.reshape(context_size, row_count, -1), "ctx", 0, 0)
    projected = jnp.sum(partial.astype(jnp.float32), axis=0).astype(jnp.bfloat16)[None]
    return projected, to_rows(grad_q), to_rows(grad_k), to_rows(grad_v)


def aligned(mesh, query_shape, weight_shape):
    devices = mesh.shape["fsdp"] * mesh.shape["ctx"]
    return (weight_shape[1] // devices) % HEAD_SIZE == 0 and query_shape[1] <= 2048


def solution(mesh):
    placed = (
        P("fsdp", "ctx", None),
        P("fsdp", "ctx", None),
        P("fsdp", "ctx", None),
        P("fsdp", "ctx"),
        P(None, ("fsdp", "ctx"), None),
        P("fsdp", "ctx", None),
    )
    def whole(*arrays):
        local = per_device if aligned(mesh, arrays[0].shape, arrays[4].shape) else per_device_gathered
        return jax.shard_map(
            local,
            mesh=mesh,
            in_specs=placed,
            out_specs=(P("fsdp", "ctx", None),) * 4,
            check_vma=False,
        )(*arrays)

    return whole
```

```python
import jax
import jax.numpy as jnp
from jax import lax
from jax.experimental import pallas as pl
from jax.experimental.pallas import tpu as pltpu
from jax.sharding import PartitionSpec as P

HEAD_SIZE = 128


def block_count(length):
    return max(1, min(8, length // 512))


def probabilities(query_block, key_prefix, offset):
    scaling = query_block.shape[-1] ** (-0.5)
    scores = (
        jnp.einsum("hqd,hkd->hqk", query_block, key_prefix, preferred_element_type=jnp.float32)
        * scaling
    )
    query_places = offset + jnp.arange(query_block.shape[1])
    key_places = jnp.arange(key_prefix.shape[1])
    scores = jnp.where(key_places[None, None, :] <= query_places[None, :, None], scores, -jnp.inf)
    highest = jnp.max(scores, axis=-1, keepdims=True)
    raised = jnp.exp(scores - highest)
    return raised / jnp.sum(raised, axis=-1, keepdims=True)


def attend_forward(queries, keys_all, values_all):
    length = queries.shape[1]
    block_rows = length // block_count(length)
    pieces = []
    for block_index in range(length // block_rows):
        offset = block_index * block_rows
        finish = offset + block_rows
        weights = probabilities(queries[:, offset:finish], keys_all[:, :finish], offset).astype(
            jnp.bfloat16
        )
        output = jnp.einsum(
            "hqk,hkd->hqd", weights, values_all[:, :finish], preferred_element_type=jnp.float32
        )
        pieces.append(output.astype(jnp.bfloat16))
    return jnp.concatenate(pieces, axis=1)


def attend_backward(queries, keys_all, values_all, attention, grad_attention):
    length = queries.shape[1]
    block_rows = length // block_count(length)
    scaling = queries.shape[-1] ** (-0.5)
    grad_keys = jnp.zeros(queries.shape, jnp.float32)
    grad_values = jnp.zeros(queries.shape, jnp.float32)
    query_pieces = []
    for block_index in range(length // block_rows):
        offset = block_index * block_rows
        finish = offset + block_rows
        query_block = queries[:, offset:finish]
        weights = probabilities(query_block, keys_all[:, :finish], offset)
        grad_block = grad_attention[:, offset:finish]
        attn_block = attention[:, offset:finish]
        grad_values = grad_values.at[:, :finish].add(
            jnp.einsum(
                "hqk,hqd->hkd",
                weights.astype(jnp.bfloat16),
                grad_block,
                preferred_element_type=jnp.float32,
            )
        )
        grad_weights = jnp.einsum(
            "hqd,hkd->hqk", grad_block, values_all[:, :finish], preferred_element_type=jnp.float32
        )
        row_delta = jnp.sum(
            grad_block.astype(jnp.float32) * attn_block.astype(jnp.float32), axis=-1, keepdims=True
        )
        grad_scores = (weights * (grad_weights - row_delta) * scaling).astype(jnp.bfloat16)
        query_pieces.append(
            jnp.einsum(
                "hqk,hkd->hqd",
                grad_scores,
                keys_all[:, :finish],
                preferred_element_type=jnp.float32,
            ).astype(jnp.bfloat16)
        )
        grad_keys = grad_keys.at[:, :finish].add(
            jnp.einsum("hqk,hqd->hkd", grad_scores, query_block, preferred_element_type=jnp.float32)
        )
    return (
        jnp.concatenate(query_pieces, axis=1),
        grad_keys.astype(jnp.bfloat16),
        grad_values.astype(jnp.bfloat16),
    )


def transposed_product(left, right):
    return lax.dot_general(
        left, right, (((1,), (1,)), ((), ())), preferred_element_type=jnp.float32
    )


def heads_first(flat, length, local_heads):
    return flat.reshape(length, local_heads, HEAD_SIZE).transpose(1, 0, 2)


def heads_last(stacked, length, local_width):
    return stacked.transpose(1, 0, 2).reshape(1, length, local_width)


def per_device_gathered(query_proj, key_proj, value_proj, modality, out_weight, grad_projected):
    context_size = lax.axis_size("ctx")
    row_count = query_proj.shape[1]
    inner_width = query_proj.shape[2]
    length = row_count * context_size
    local_width = inner_width // context_size
    local_heads = local_width // HEAD_SIZE
    head_query, head_key, head_value = (
        lax.all_to_all(query_proj, "ctx", split_axis=2, concat_axis=1, tiled=True),
        lax.all_to_all(key_proj, "ctx", split_axis=2, concat_axis=1, tiled=True),
        lax.all_to_all(value_proj, "ctx", split_axis=2, concat_axis=1, tiled=True),
    )
    head_query = heads_first(head_query, length, local_heads)
    head_key = heads_first(head_key, length, local_heads)
    head_value = heads_first(head_value, length, local_heads)
    attention = attend_forward(head_query, head_key, head_value)
    sending = heads_last(attention, length, local_width)
    attn_rows = lax.all_to_all(sending, "ctx", split_axis=1, concat_axis=2, tiled=True)[0]
    upstream = grad_projected[0]
    weight_piece = lax.all_gather(out_weight, ("fsdp", "ctx"), axis=1, tiled=True)
    text_out = jnp.dot(attn_rows, weight_piece[0], preferred_element_type=jnp.float32)
    image_out = jnp.dot(attn_rows, weight_piece[1], preferred_element_type=jnp.float32)
    text_grad = transposed_product(upstream, weight_piece[0])
    image_grad = transposed_product(upstream, weight_piece[1])
    text_out, image_out, text_grad, image_grad = (text_out, image_out, text_grad, image_grad)
    image_rows = (modality[0] == 1)[:, None]
    projected = jnp.where(image_rows, image_out, text_out).astype(jnp.bfloat16)[None]
    grad_rows = jnp.where(image_rows, image_grad, text_grad).astype(jnp.bfloat16)
    grad_heads = lax.all_to_all(grad_rows[None], "ctx", split_axis=2, concat_axis=1, tiled=True)
    grad_heads = heads_first(grad_heads, length, local_heads)
    grad_q, grad_k, grad_v = attend_backward(
        head_query, head_key, head_value, attention, grad_heads
    )
    grad_query, grad_key, grad_value = (
        lax.all_to_all(
            heads_last(grad_q, length, local_width), "ctx", split_axis=1, concat_axis=2, tiled=True
        ),
        lax.all_to_all(
            heads_last(grad_k, length, local_width), "ctx", split_axis=1, concat_axis=2, tiled=True
        ),
        lax.all_to_all(
            heads_last(grad_v, length, local_width), "ctx", split_axis=1, concat_axis=2, tiled=True
        ),
    )
    return (projected, grad_query, grad_key, grad_value)


def fused_attention_kernel(
    q_ref, k_ref, v_ref, g_ref, a_ref, dq_ref, dk_ref, dv_ref, dk_sum, dv_sum
):
    length = q_ref.shape[0]
    rows = min(256, length)
    scaling = HEAD_SIZE ** (-0.5)
    nt = (((1,), (1,)), ((), ()))
    tn = (((0,), (0,)), ((), ()))
    for block in reversed(range(length // rows)):
        offset = block * rows
        finish = offset + rows
        q = q_ref[offset:finish, :]
        g = g_ref[offset:finish, :]
        k = k_ref[:finish, :]
        v = v_ref[:finish, :]
        scores = lax.dot_general(q, k, nt, preferred_element_type=jnp.float32) * scaling
        places = lax.broadcasted_iota(jnp.int32, scores.shape, 0) + offset
        scores = jnp.where(
            lax.broadcasted_iota(jnp.int32, scores.shape, 1) <= places, scores, -jnp.inf
        )
        raised = jnp.exp(scores - jnp.max(scores, axis=-1, keepdims=True))
        weights = raised * (1.0 / jnp.sum(raised, axis=-1, keepdims=True))
        weights_bf = weights.astype(jnp.bfloat16)
        attention = jnp.dot(weights_bf, v, preferred_element_type=jnp.float32).astype(jnp.bfloat16)
        a_ref[offset:finish, :] = attention
        delta = jnp.sum(
            g.astype(jnp.float32) * attention.astype(jnp.float32), axis=-1, keepdims=True
        )
        grad_weights = lax.dot_general(g, v, nt, preferred_element_type=jnp.float32)
        grad_scores = (weights * (grad_weights - delta) * scaling).astype(jnp.bfloat16)
        dq_ref[offset:finish, :] = jnp.dot(
            grad_scores, k, preferred_element_type=jnp.float32
        ).astype(jnp.bfloat16)
        dk = lax.dot_general(grad_scores, q, tn, preferred_element_type=jnp.float32)
        dv = lax.dot_general(weights_bf, g, tn, preferred_element_type=jnp.float32)
        if finish == length:
            dk_sum[...] = dk
            dv_sum[...] = dv
        else:
            dk_sum[:finish, :] += dk
            dv_sum[:finish, :] += dv
    dk_ref[...] = dk_sum[...].astype(jnp.bfloat16)
    dv_ref[...] = dv_sum[...].astype(jnp.bfloat16)


def fused_attention(q, k, v, g):
    length, width = q.shape
    spec = pl.BlockSpec((length, HEAD_SIZE), lambda h: (0, h))
    return pl.pallas_call(
        fused_attention_kernel,
        grid=(width // HEAD_SIZE,),
        in_specs=[spec] * 4,
        out_specs=[spec] * 4,
        out_shape=[jax.ShapeDtypeStruct(q.shape, jnp.bfloat16)] * 4,
        scratch_shapes=[pltpu.VMEM((length, HEAD_SIZE), jnp.float32)] * 2,
        compiler_params=pltpu.CompilerParams(vmem_limit_bytes=48 * 2**20),
        cost_estimate=pl.CostEstimate(
            flops=9 * length * length * width, bytes_accessed=16 * length * width, transcendentals=0
        ),
    )(q, k, v, g)


def exchange(arrays, kinds, collective_id):
    size, groups = lax.axis_size("ctx"), lax.axis_size("fsdp")
    places = size // 2
    spans = {
        "deal": size, "ctx": size, "chain": size, "fsdp": groups, "line": places, "swap": 2
    }
    count = len(arrays)

    def block_shape(a, kind):
        if kind in ("deal", "line"):
            return a.shape[1:]
        return (a.shape[0], *a.shape[2:]) if kind == "swap" else a.shape

    blocks = [block_shape(a, kind) for a, kind in zip(arrays, kinds)]
    slots = max(size, groups)

    def body(*refs):
        sources, targets, held = refs[:count], refs[count : 2 * count], refs[2 * count : 3 * count]
        send, receive, load, store, up, down, arrive, across, landed = refs[3 * count :]
        ctx, group = lax.axis_index("ctx"), lax.axis_index("fsdp")
        place, side = ctx // 2, ctx % 2
        position = {
            "deal": ctx, "ctx": ctx, "chain": ctx, "fsdp": group, "line": place, "swap": side
        }

        def device(kind, j):
            if kind == "fsdp":
                return {"fsdp": j}
            if kind == "line":
                return {"ctx": j * 2 + side}
            return {"ctx": place * 2 + j} if kind == "swap" else {"ctx": j}

        def block(i, owner):
            if kinds[i] in ("deal", "line"):
                return sources[i].at[owner]
            return sources[i].at[:, owner] if kinds[i] == "swap" else sources[i]

        def remote(source, target, send_sem, receive_sem, device_id):
            return pltpu.make_async_remote_copy(
                src_ref=source,
                dst_ref=target,
                send_sem=send_sem,
                recv_sem=receive_sem,
                device_id=device_id,
                device_id_type=pl.DeviceIdType.MESH,
            )

        own = [
            pltpu.make_async_copy(block(i, position[kinds[i]]), held[i], load.at[i])
            for i in range(count)
        ]
        for copy in own:
            copy.start()
        barrier = pltpu.get_barrier_semaphore()
        greeted = [({"ctx": lax.rem(ctx + step, size)}) for step in range(1, size)]
        if "fsdp" in kinds:
            greeted += [{"fsdp": lax.rem(group + step, groups)} for step in range(1, groups)]
        for peer in greeted:
            pl.semaphore_signal(barrier, 1, device_id=peer, device_id_type=pl.DeviceIdType.MESH)
        pl.semaphore_wait(barrier, len(greeted))

        copies = []

        def spread(i):
            kind = kinds[i]
            for step in range(1, spans[kind]):
                peer = lax.rem(position[kind] + step, spans[kind])
                copy = remote(
                    block(i, peer),
                    targets[i].at[position[kind]],
                    send.at[i, step],
                    receive.at[i, step],
                    device(kind, peer),
                )
                copy.start()
                copies.append(copy)

        def hop(i, origin, first, ahead, sems):
            slot = targets[i].at[origin * 2 + side]
            source = sources[i] if first else slot
            return remote(
                source, slot, sems.at[origin], arrive.at[origin], {"ctx": ahead * 2 + side}
            )

        def cross(i, origin, first):
            slot = targets[i].at[origin * 2 + side]
            source = sources[i] if first else slot
            return remote(
                source, slot, across.at[origin], landed.at[origin], {"ctx": place * 2 + 1 - side}
            )

        def pass_on(i, distance, finish=False):
            first = distance == 0
            act = (lambda c: c.wait_send()) if finish else (lambda c: c.start())
            for sems, sign in ((up, 1), (down, -1)):
                origin = place - sign * distance
                ahead = place + sign
                there = (origin >= 0) & (origin < places)

                @pl.when(there)
                def _():
                    if not first and not finish:
                        hop(i, origin, first, place, sems).wait_recv()

                    @pl.when((ahead >= 0) & (ahead < places))
                    def _():
                        act(hop(i, origin, first, ahead, sems))

                    if not first or sign == 1:
                        act(cross(i, origin, first))

        chain = kinds.index("chain") if "chain" in kinds else None
        rest = [i for i in range(count) if i != chain]
        deals = [i for i in rest if kinds[i] == "deal"]
        if chain is None:
            for i in rest:
                spread(i)
        else:
            pass_on(chain, 0)
            for i in rest:
                if i not in deals:
                    spread(i)
            for turn in range(max(len(deals), places - 1)):
                if turn < len(deals):
                    spread(deals[turn])
                if turn < places - 1:
                    pass_on(chain, turn + 1)
        for i in range(count):
            own[i].wait()
            back = pltpu.make_async_copy(held[i], targets[i].at[position[kinds[i]]], store.at[i])
            back.start()
            own[i] = back
        for copy in own + copies:
            copy.wait()
        if chain is not None:
            for distance in range(places):
                pass_on(chain, distance, finish=True)
            for origin in range(places):
                slot = targets[chain].at[origin * 2 + 1 - side]
                remote(
                    slot, slot, across.at[origin], landed.at[origin], {"ctx": place * 2 + 1 - side}
                ).wait_recv()

    return pl.pallas_call(
        body,
        in_specs=[pl.BlockSpec(memory_space=pl.ANY)] * count,
        out_specs=[pl.BlockSpec(memory_space=pl.ANY)] * count,
        out_shape=[
            jax.ShapeDtypeStruct((spans[kind], *block), a.dtype)
            for a, kind, block in zip(arrays, kinds, blocks)
        ],
        scratch_shapes=[pltpu.VMEM(block, a.dtype) for a, block in zip(arrays, blocks)]
        + [pltpu.SemaphoreType.DMA((count, slots))] * 2
        + [pltpu.SemaphoreType.DMA((count,))] * 2
        + [pltpu.SemaphoreType.DMA((places,))] * 5,
        compiler_params=pltpu.CompilerParams(collective_id=collective_id, has_side_effects=True),
    )(*arrays)


def per_device(query_proj, key_proj, value_proj, modality, out_weight, grad_projected):
    context_size = lax.axis_size("ctx")
    groups = lax.axis_size("fsdp")
    row_count = query_proj.shape[1]
    piece = out_weight.shape[1]
    length = row_count * context_size
    width = groups * piece

    def to_heads(flat):
        return flat[0].reshape(row_count, groups, context_size, piece).transpose(2, 0, 1, 3).reshape(
            context_size, row_count, width
        )

    def to_rows(blocks):
        split = blocks.reshape(context_size, row_count, groups, piece)
        return split.transpose(1, 2, 0, 3).reshape(1, row_count, width * context_size)

    marks = jnp.broadcast_to(modality, (8, row_count))
    weight, upstream, marks, query, key, value = exchange(
        (
            out_weight,
            grad_projected[0],
            marks,
            to_heads(query_proj),
            to_heads(key_proj),
            to_heads(value_proj),
        ),
        ("fsdp", "chain", "ctx", "deal", "deal", "deal"),
        0,
    )
    image = (marks[:, 0, :] == 1).reshape(length, 1)
    upstream = upstream.reshape(length, -1)
    weight = weight.reshape(groups * 2 * piece, -1)
    both = transposed_product(upstream, weight).reshape(length, groups, 2, piece)
    grad_attention = (
        jnp.where(image[:, :, None], both[:, :, 1], both[:, :, 0])
        .reshape(length, width)
        .astype(jnp.bfloat16)
    )
    attention, grad_q, grad_k, grad_v = fused_attention(
        query.reshape(length, width),
        key.reshape(length, width),
        value.reshape(length, width),
        grad_attention,
    )
    spread = attention.reshape(length, groups, piece)
    zero = jnp.zeros_like(spread)
    spread = jnp.stack(
        [jnp.where(image[:, :, None], zero, spread), jnp.where(image[:, :, None], spread, zero)],
        axis=2,
    ).reshape(length, 2 * width)
    partial = jnp.dot(spread, weight, preferred_element_type=jnp.float32).astype(jnp.bfloat16)
    halves, grad_q, grad_k, grad_v = exchange(
        [partial.reshape(context_size // 2, 2, row_count, -1)]
        + [a.reshape(context_size, row_count, -1) for a in (grad_q, grad_k, grad_v)],
        ("swap", "deal", "deal", "deal"),
        1,
    )
    half = jnp.sum(halves.astype(jnp.float32), axis=0).astype(jnp.bfloat16)
    (partial,) = exchange([half], ("line",), 2)
    projected = jnp.sum(partial.astype(jnp.float32), axis=0).astype(jnp.bfloat16)[None]
    return projected, to_rows(grad_q), to_rows(grad_k), to_rows(grad_v)


def aligned(mesh, query_shape, weight_shape):
    devices = mesh.shape["fsdp"] * mesh.shape["ctx"]
    return (weight_shape[1] // devices) % HEAD_SIZE == 0 and query_shape[1] <= 2048 and mesh.shape["ctx"] % 2 == 0


def solution(mesh):
    placed = (
        P("fsdp", "ctx", None),
        P("fsdp", "ctx", None),
        P("fsdp", "ctx", None),
        P("fsdp", "ctx"),
        P(None, ("fsdp", "ctx"), None),
        P("fsdp", "ctx", None),
    )
    def whole(*arrays):
        local = per_device if aligned(mesh, arrays[0].shape, arrays[4].shape) else per_device_gathered
        return jax.shard_map(
            local,
            mesh=mesh,
            in_specs=placed,
            out_specs=(P("fsdp", "ctx", None),) * 4,
            check_vma=False,
        )(*arrays)

    return whole
```
